32 devices in a mesh: frames: 2 (over x), chain: 16 (over z, y, core).
Axes of the slice: x: 2, y: 2, z: 4, core: 2. Of those that a mesh axis runs over, the one named last changes fastest.
Arguments:
- species: int32 [8192], P(('frames', 'chain')), parts along dimension 0, may hold values from 0 to 127
- positions: float32 [3, 8192], P(None, ('frames', 'chain')), parts along dimension 1, may hold values from -18 to 18
- block_list: int32 [64, 3], P(('frames', 'chain')), parts along dimension 0, may hold values from -1 to 31, as said below
- embed_table: bfloat16 [128, 512], replicated, may hold values from -6 to 6
- w_query: bfloat16 [2, 512, 512], replicated, may hold values from -0.25 to 0.25
- w_key: bfloat16 [2, 512, 512], replicated, may hold values from -0.25 to 0.25
- w_value: bfloat16 [2, 512, 512], replicated, may hold values from -0.25 to 0.25
- w_out: bfloat16 [2, 512, 512], replicated, may hold values from -0.25 to 0.25
- w_up: bfloat16 [2, 512, 1024], replicated, may hold values from -0.25 to 0.25
- w_down: bfloat16 [2, 1024, 512], replicated, may hold values from -0.1875 to 0.1875
- norm_gains: float32 [2, 2, 512], replicated, may hold values from 0.5 to 1.5
- gammas: float32 [2, 16], replicated, may hold values from 0.005 to 0.1
- out_gain: float32 [512], replicated, may hold values from 0.5 to 1.5
- readout: float32 [512], replicated, may hold values from -0.25 to 0.25
Outputs:
- energy: float32 [2], P('frames'), parts along dimension 0
- forces: float32 [3, 8192], P(None, ('frames', 'chain')), parts along dimension 1
The draws below stay inside these ranges and needn't reach their ends.
There are 2 independent parts, one for each index of `frames`. The reference program is written for one: setup_inputs(seed, part) draws one part's arguments, and reference() takes and returns one part's arrays. A program takes and returns all parts, laid end to end along the dimension named above; an argument that names none is the same for every part. Nothing has to cross between parts.
Inputs may be any that keep to these rules, and one draw needn't show every extreme that they name: `block_list`: row b holds b-1 or -1, then b, then b+1 or -1; -1 marks a neighbouring block outside the cutoff.
All inputs are finite; a program needn't handle non-finite values.
Results may differ from the reference program's by a relative error of at most 0.022.
Values may be sent and summed in bfloat16 or wider, within the bound.
A program may use at most 128 MiB of HBM per device.

```python
import math
import jax
import jax.numpy as jnp
from jax import lax

D = 512
HEADS = 16
FF = 1024
NSPEC = 128
LAYERS = 2
BLOCKS = 32
ATOMS = 4096


def draw_block_list(key, part):
    ids = jnp.arange(BLOCKS, dtype=jnp.int32)
    key_left, key_right = jax.random.split(jax.random.fold_in(key, 7))
    left = jax.random.randint(key_left, (BLOCKS,), 0, 5) < 3
    right = jax.random.randint(key_right, (BLOCKS,), 0, 5) < 3
    lower = jnp.where(left & (ids > 0), ids - 1, -1)
    upper = jnp.where(right & (ids < BLOCKS - 1), ids + 1, -1)
    return jnp.stack([lower, ids, upper], axis=1).astype(jnp.int32)


def touch_ends(array, own_key, low, largest):
    longest = array.shape.index(max(array.shape))
    spots = []
    for shift in (0, 1):
        where = [jax.random.randint(jax.random.fold_in(own_key, axis), (), 0, length) for axis, length in enumerate(array.shape)]
        where[longest] = (where[longest] + shift) % array.shape[longest]
        spots.append(tuple(where))
    return array.at[spots[0]].set(low).at[spots[1]].set(largest)


def shard_levels(key, shape, shards, smallest, largest):
    def one(axis_at, blocks):
        draws = jax.random.uniform(jax.random.fold_in(jax.random.fold_in(key, 6), axis_at), (blocks,), jnp.float32, smallest / len(shards), largest / len(shards))
        return jnp.repeat(jnp.exp(draws), shape[axis_at] // blocks).reshape((-1,) + (1,) * (len(shape) - axis_at - 1))

    level = one(*shards[0])
    for cut in shards[1:]:
        level = level * one(*cut)
    return level


def gaussian(own_key, extent, scale, bound, cuts=(), held_as=jnp.bfloat16):
    values = scale * jax.random.normal(own_key, extent, jnp.float32)
    if cuts:
        values = values * shard_levels(own_key, extent, cuts, -0.22, 0.18)
    return jnp.clip(values, -bound, bound).astype(held_as)


def setup_inputs(seed: int = 0, part: int = 0) -> dict:
    key_list = jax.random.split(jax.random.key(seed), 15)
    part_keys = jax.random.split(jax.random.fold_in(key_list[14], part), 15)
    species = touch_ends(jax.random.randint(part_keys[0], (ATOMS,), 0, NSPEC), jax.random.fold_in(part_keys[0], 1), 0, NSPEC - 1).astype(jnp.int32)
    positions = gaussian(part_keys[1], (3, ATOMS), 3.0, 18.0, ((1, 16),), jnp.float32)
    block_list = draw_block_list(jax.random.fold_in(jax.random.fold_in(key_list[14], part), 71), part)
    embed_table = gaussian(key_list[3], (NSPEC, D), 1.0, 6.0)
    w_query = gaussian(key_list[4], (LAYERS, D, D), D ** -0.5, 0.25)
    w_key = gaussian(key_list[5], (LAYERS, D, D), D ** -0.5, 0.25)
    w_value = gaussian(key_list[6], (LAYERS, D, D), D ** -0.5, 0.25)
    w_out = gaussian(key_list[7], (LAYERS, D, D), D ** -0.5, 0.25)
    w_up = gaussian(key_list[8], (LAYERS, D, FF), D ** -0.5, 0.25)
    w_down = gaussian(key_list[9], (LAYERS, FF, D), FF ** -0.5, 0.1875)
    norm_gains = jnp.clip(1.0 + 0.1 * jax.random.normal(key_list[10], (LAYERS, 2, D), jnp.float32), 0.5, 1.5)
    gammas = jnp.clip(jnp.exp(jax.random.uniform(key_list[11], (LAYERS, HEADS), jnp.float32, math.log(0.005), math.log(0.1))), 0.005, 0.1)
    out_gain = jnp.clip(1.0 + 0.1 * jax.random.normal(key_list[12], (D,), jnp.float32), 0.5, 1.5)
    readout = gaussian(key_list[13], (D,), D ** -0.5, 0.25, (), jnp.float32)
    return {"species": species, "positions": positions, "block_list": block_list, "embed_table": embed_table, "w_query": w_query, "w_key": w_key, "w_value": w_value, "w_out": w_out, "w_up": w_up, "w_down": w_down, "norm_gains": norm_gains, "gammas": gammas, "out_gain": out_gain, "readout": readout}


def rms(x, gain):
    return x * lax.rsqrt(lax.optimization_barrier(jnp.mean(x * x, axis=-1, keepdims=True)) + 1e-06) * gain

def windows(ext, nblk):
    blocks = ext.reshape(nblk + 2, 128, ext.shape[-1])
    return jnp.concatenate([blocks[:-2], blocks[1:-1], blocks[2:]], axis=1)

def attend(query, key_ext, value_ext, coord, coord_ext, valid, gamma, heads):
    atoms, width = query.shape
    nblk = atoms // 128
    hdim = width // heads
    key_win = windows(key_ext, nblk).astype(jnp.bfloat16).reshape(nblk, 384, heads, hdim)
    value_win = windows(value_ext, nblk).astype(jnp.bfloat16).reshape(nblk, 384, heads, hdim)
    query_blk = query.reshape(nblk, 128, heads, hdim)
    scores = jnp.einsum('bqhd,bkhd->bhqk', query_blk.astype(jnp.float32), key_win.astype(jnp.float32), precision=lax.Precision.HIGHEST) * hdim ** (-0.5)
    coord_blk = coord_ext.reshape(3, nblk + 2, 128)
    coord_win = jnp.concatenate([coord_blk[:, :-2], coord_blk[:, 1:-1], coord_blk[:, 2:]], axis=2)
    coord_q = coord.reshape(3, nblk, 128)
    dist_sq = lax.optimization_barrier(jnp.sum((coord_q[:, :, :, None] - coord_win[:, :, None, :]) ** 2, axis=0))
    scores = scores - gamma[None, :, None, None] * dist_sq[:, None]
    keymask = jnp.repeat(valid, 128, axis=1)
    scores = jnp.where(keymask[:, None, None, :], scores, -1e+30)
    peak = lax.stop_gradient(lax.optimization_barrier(jnp.max(scores, axis=-1, keepdims=True)))
    expo = jnp.exp(scores - peak)
    probs = (expo / lax.optimization_barrier(jnp.sum(expo, axis=-1, keepdims=True))).astype(jnp.bfloat16)
    mixed = jnp.einsum('bhqk,bkhd->bqhd', probs.astype(jnp.float32), value_win.astype(jnp.float32), precision=lax.Precision.HIGHEST)
    return mixed.reshape(atoms, width).astype(jnp.bfloat16)

def energy_of(positions, species, valid, embed_table, w_query, w_key, w_value, w_out, w_up, w_down, norm_gains, gammas, out_gain, readout):
    heads = gammas.shape[1]
    onehot = jax.nn.one_hot(species, embed_table.shape[0], dtype=jnp.bfloat16)
    state = jnp.dot(onehot, embed_table, preferred_element_type=jnp.float32)
    for layer in range(w_query.shape[0]):
        normed = rms(state, norm_gains[layer, 0]).astype(jnp.bfloat16)
        query = jnp.dot(normed, w_query[layer], preferred_element_type=jnp.float32).astype(jnp.bfloat16)
        keys = jnp.dot(normed, w_key[layer], preferred_element_type=jnp.float32).astype(jnp.bfloat16)
        values = jnp.dot(normed, w_value[layer], preferred_element_type=jnp.float32).astype(jnp.bfloat16)
        key_ext = jnp.pad(keys.astype(jnp.float32), ((128, 128), (0, 0)))
        value_ext = jnp.pad(values.astype(jnp.float32), ((128, 128), (0, 0)))
        coord_ext = jnp.pad(positions, ((0, 0), (128, 128)))
        att = attend(query, key_ext, value_ext, positions, coord_ext, valid, gammas[layer], heads)
        state = state + jnp.dot(att, w_out[layer], preferred_element_type=jnp.float32)
        inner = rms(state, norm_gains[layer, 1]).astype(jnp.bfloat16)
        hidden = jax.nn.gelu(jnp.dot(inner, w_up[layer], preferred_element_type=jnp.float32)).astype(jnp.bfloat16)
        state = state + jnp.dot(hidden, w_down[layer], preferred_element_type=jnp.float32)
    per_atom = jnp.dot(rms(state, out_gain), readout, precision=lax.Precision.HIGHEST)
    return jnp.sum(per_atom)

def reference(species, positions, block_list, embed_table, w_query, w_key, w_value, w_out, w_up, w_down, norm_gains, gammas, out_gain, readout):
    nblk = block_list.shape[0]
    ids = jnp.arange(nblk, dtype=jnp.int32)
    expect = ids[:, None] - 1 + jnp.arange(3, dtype=jnp.int32)[None, :]
    valid = (block_list == expect) & (block_list >= 0)

    def total(coords):
        return energy_of(coords, species, valid, embed_table, w_query, w_key, w_value, w_out, w_up, w_down, norm_gains, gammas, out_gain, readout)
    value, pullback = jax.vjp(total, positions)
    grad, = pullback(jnp.ones((), value.dtype))
    return (value.reshape(1), -grad)
```

```python
import functools
import math

import jax
import jax.numpy as jnp
from jax import lax
from jax.experimental import pallas as pl
from jax.experimental.pallas import tpu as pltpu
from jax.sharding import PartitionSpec as P

MESH = pl.DeviceIdType.MESH
BLOCK = 128
LANES = 128
FAR = 1e30
EPS = 1e-06
GELU_A = math.sqrt(2.0 / math.pi)
GELU_B = 0.044715
F32 = jnp.float32
BF16 = jnp.bfloat16


def mm(a, b):
    return jnp.dot(a, b, preferred_element_type=F32)


def mm_nt(a, b):
    return lax.dot_general(a, b, (((1,), (1,)), ((), ())), preferred_element_type=F32)


def mm_tn(a, b):
    return lax.dot_general(a, b, (((0,), (0,)), ((), ())), preferred_element_type=F32)


def inv_rms(x):
    return lax.rsqrt(jnp.mean(x * x, axis=-1, keepdims=True) + EPS)


def rms_back(x, gain, dy):
    r = inv_rms(x)
    gy = gain * dy
    return r * gy - x * (r * r * r * jnp.mean(x * gy, axis=-1, keepdims=True))


def gelu(x):
    return 0.5 * x * (1.0 + jnp.tanh(GELU_A * (x + GELU_B * x * x * x)))


def gelu_slope(x):
    sq = x * x
    t = jnp.tanh(GELU_A * x * (1.0 + GELU_B * sq))
    return 0.5 * (1.0 + t) + (0.5 * GELU_A) * x * (1.0 - t * t) * (1.0 + 3.0 * GELU_B * sq)


def kernel(
    chain, nblk, layers, heads,
    spec_ref, pos_ref, blk_ref, gam_ref, gains_ref, og_ref, ro_ref, table_ref,
    wq_any, wk_any, wv_any, wo_any, wu_any, wd_any,
    e_ref, f_ref,
    wq, wk, wv, wo, wu, wd,
    sp_lo, sp_hi, ps_lo, ps_hi,
    xn, qs, ks, vs, kt, vt, probs, dist, gsum,
    att, xin, xmid, pre, dacc, dat, dqt, dks, dvs,
    gsend, grecv, fsend, frecv, fown, esend, erecv,
    wsem, ssem, rsem, essem, ersem,
):
    atoms = pos_ref.shape[1]
    width = table_ref.shape[1]
    nspec = table_ref.shape[0]
    hdim = width // heads
    per = LANES // hdim
    groups = width // LANES
    win = 3 * BLOCK
    ext = atoms + 2 * BLOCK
    own = slice(BLOCK, BLOCK + atoms)
    scale = hdim ** -0.5
    me = lax.axis_index("chain")
    has_l = me > 0
    has_r = me < chain - 1
    left = lax.rem(me + chain - 1, chain)
    right = lax.rem(me + 1, chain)
    steps = chain.bit_length() - 1

    loads = {}
    for layer in range(layers):
        for i, (src, dst) in enumerate(
            ((wk_any, wk), (wv_any, wv), (wq_any, wq), (wo_any, wo), (wu_any, wu), (wd_any, wd))
        ):
            copy = pltpu.make_async_copy(src.at[layer], dst.at[layer], wsem.at[layer, i])
            copy.start()
            loads[layer, i] = copy

    barrier = pltpu.get_barrier_semaphore()
    partners = []
    for s in range(steps):
        bit = 1 << s
        partners.append(me + bit - 2 * bit * lax.rem(lax.div(me, bit), 2))

    def greet(to):
        pl.semaphore_signal(barrier, inc=1, device_id={"chain": to}, device_id_type=MESH)

    for partner in partners[1:]:
        greet(partner)

    @pl.when(has_l)
    def _():
        greet(left)

    @pl.when(has_r)
    def _():
        greet(right)

    pl.semaphore_wait(
        barrier, max(0, steps - 1) + has_l.astype(jnp.int32) + has_r.astype(jnp.int32)
    )

    def swap(slot, first, last, high, low):
        to_left = pltpu.make_async_remote_copy(
            src_ref=first, dst_ref=high, send_sem=ssem.at[slot, 0], recv_sem=rsem.at[slot, 0],
            device_id={"chain": left}, device_id_type=MESH,
        )
        to_right = pltpu.make_async_remote_copy(
            src_ref=last, dst_ref=low, send_sem=ssem.at[slot, 1], recv_sem=rsem.at[slot, 1],
            device_id={"chain": right}, device_id_type=MESH,
        )
        return to_left, to_right

    def start(pair):
        pl.when(has_l)(pair[0].start)
        pl.when(has_r)(pair[1].start)

    def received(pair):
        pl.when(has_r)(pair[0].wait_recv)
        pl.when(has_l)(pair[1].wait_recv)

    def sent(pair):
        pl.when(has_l)(pair[0].wait_send)
        pl.when(has_r)(pair[1].wait_send)

    head_first = pl.ds(0, BLOCK)
    head_last = pl.ds(atoms - BLOCK, BLOCK)
    swap_sp = swap(0, spec_ref.at[:, head_first], spec_ref.at[:, head_last], sp_hi, sp_lo)
    swap_ps = swap(1, pos_ref.at[:, head_first], pos_ref.at[:, head_last], ps_hi, ps_lo)
    start(swap_sp)
    start(swap_ps)
    swap_xn = swap(
        2,
        xn.at[1, pl.ds(BLOCK, BLOCK)], xn.at[1, pl.ds(atoms, BLOCK)],
        xn.at[1, pl.ds(BLOCK + atoms, BLOCK)], xn.at[1, pl.ds(0, BLOCK)],
    )
    swap_g = swap(3, gsend.at[0], gsend.at[1], grecv.at[1], grecv.at[0])
    swap_f = swap(4, fsend.at[0], fsend.at[1], frecv.at[1], frecv.at[0])

    @pl.when(me == 0)
    def _():
        sp_lo[...] = jnp.zeros_like(sp_lo)
        ps_lo[...] = jnp.zeros_like(ps_lo)
        xn[1, 0:BLOCK, :] = jnp.zeros((BLOCK, width), BF16)
        grecv[0] = jnp.zeros((BLOCK, width), BF16)
        frecv[0] = jnp.zeros((8, BLOCK), F32)

    @pl.when(me == chain - 1)
    def _():
        sp_hi[...] = jnp.zeros_like(sp_hi)
        ps_hi[...] = jnp.zeros_like(ps_hi)
        xn[1, BLOCK + atoms : ext, :] = jnp.zeros((BLOCK, width), BF16)
        grecv[1] = jnp.zeros((BLOCK, width), BF16)
        frecv[1] = jnp.zeros((8, BLOCK), F32)

    table = table_ref[...]

    def embed(row):
        count = row.shape[1]
        hot = (lax.broadcasted_iota(jnp.int32, (nspec, count), 0) == row).astype(F32).astype(BF16)
        return mm_tn(hot, table)

    def norm(x, gain):
        return (x * inv_rms(x) * gain).astype(BF16)

    gain_a = [gains_ref[layer, 0:1, :] for layer in range(layers)]
    gain_b = [gains_ref[layer, 1:2, :] for layer in range(layers)]

    state = embed(spec_ref[...])
    xn[0, own, :] = norm(state, gain_a[0])
    received(swap_sp)
    xn[0, 0:BLOCK, :] = norm(embed(sp_lo[...]), gain_a[0])
    xn[0, BLOCK + atoms : ext, :] = norm(embed(sp_hi[...]), gain_a[0])
    received(swap_ps)

    rows = [ps_lo] + [pos_ref.at[:, pl.ds(b * BLOCK, BLOCK)] for b in range(nblk)] + [ps_hi]
    columns = [
        [jnp.transpose(jnp.broadcast_to(ref[c : c + 1, :], (BLOCK, BLOCK))) for c in range(3)]
        for ref in rows
    ]
    for b in range(nblk):
        for s in range(3):
            total = None
            for c in range(3):
                diff = columns[b + s][c] - rows[b + 1][c : c + 1, :]
                total = diff * diff if total is None else total + diff * diff
            block = blk_ref[b, s]
            listed = jnp.logical_and(block == me * nblk + (b - 1 + s), block >= 0)
            dist[b, s * BLOCK : (s + 1) * BLOCK, :] = jnp.where(listed, total, FAR)

    lane = lax.broadcasted_iota(jnp.int32, (1, LANES), 1)
    masks = [
        jnp.logical_and(lane >= i * hdim, lane < (i + 1) * hdim).astype(F32).astype(BF16)
        for i in range(per)
    ]
    gsum[...] = jnp.zeros_like(gsum)

    def keys_values(layer, part):
        src = xn[layer, part, :]
        k = mm(src, wk[layer])
        v = mm(src, wv[layer])
        ks[layer, part, :] = k.astype(BF16)
        vs[layer, part, :] = v.astype(BF16)
        vt[:, part] = jnp.transpose(v).astype(BF16)
        if layer:
            kt[:, part] = jnp.transpose(k).astype(BF16)

    def attend(layer):
        def body(g, carry):
            lanes = pl.ds(pl.multiple_of(g * LANES, LANES), LANES)
            for b in range(nblk):
                key = ks[layer, b * BLOCK : b * BLOCK + win, lanes]
                query = qs[layer, b * BLOCK : (b + 1) * BLOCK, lanes]
                far = dist[b]
                for i in range(per):
                    h = g * per + i
                    score = mm_nt(key, query * masks[i]) - (gam_ref[layer, h] / scale) * far
                    peak = jnp.max(score, axis=0, keepdims=True)
                    expo = jnp.exp2((score - peak) * (scale * math.log2(math.e)))
                    inv = 1.0 / jnp.sum(expo, axis=0, keepdims=True)
                    p = (expo * inv).astype(BF16)
                    probs[layer, h, b] = p
                    part = pl.ds(pl.multiple_of(h * hdim, hdim), hdim)
                    att[layer, part, b * BLOCK : (b + 1) * BLOCK] = mm(
                        vt[part, b * BLOCK : b * BLOCK + win], p
                    )
            return carry

        lax.fori_loop(0, groups, body, 0)

    for layer in range(layers):
        xin[layer] = state
        if layer == 0:
            loads[layer, 0].wait()
            loads[layer, 1].wait()
            keys_values(layer, slice(0, ext))
            loads[layer, 2].wait()
            qs[layer] = mm(xn[layer, own, :], wq[layer]).astype(BF16)
        else:
            xn[layer, own, :] = norm(state, gain_a[layer])
            loads[layer, 0].wait()
            loads[layer, 1].wait()
            loads[layer, 2].wait()
            start(swap_xn)
            qs[layer] = mm(xn[layer, own, :], wq[layer]).astype(BF16)
            keys_values(layer, own)
            received(swap_xn)
            keys_values(layer, slice(0, BLOCK))
            keys_values(layer, slice(BLOCK + atoms, ext))
        attend(layer)
        loads[layer, 3].wait()
        mid = state + mm(jnp.transpose(att[layer]).astype(BF16), wo[layer])
        xmid[layer] = mid
        loads[layer, 4].wait()
        hidden = mm(norm(mid, gain_b[layer]), wu[layer])
        pre[layer] = hidden
        loads[layer, 5].wait()
        state = mid + mm(gelu(hidden).astype(BF16), wd[layer])

    r = inv_rms(state)
    gy = og_ref[...] * ro_ref[...]
    energy = jnp.sum(state * r * gy)
    grad = r * gy - state * (r * r * r * jnp.mean(state * gy, axis=-1, keepdims=True))

    ecopies = [
        pltpu.make_async_remote_copy(
            src_ref=esend.at[s], dst_ref=erecv.at[s], send_sem=essem.at[s], recv_sem=ersem.at[s],
            device_id={"chain": partners[s]}, device_id_type=MESH,
        )
        for s in range(steps)
    ]
    esend[0] = jnp.broadcast_to(energy, (8, LANES))
    done = [0]

    def advance(last=False):
        s = done[0]
        if s > 0 and s <= steps:
            ecopies[s - 1].wait_recv()
            esend[s] = esend[s - 1] + erecv[s - 1]
        if s < steps:
            ecopies[s].start()
        done[0] = s + 1

    def slopes(layer, grad):
        du = mm_nt(grad.astype(BF16), wd[layer]).astype(BF16).astype(F32)
        dpre = (du * gelu_slope(pre[layer])).astype(BF16)
        dm = mm_nt(dpre, wu[layer]).astype(BF16).astype(F32)
        grad = grad + rms_back(xmid[layer], gain_b[layer], dm)
        da = mm_nt(grad.astype(BF16), wo[layer])
        dacc[...] = da.astype(BF16)
        dat[...] = jnp.transpose(da)
        return grad

    def attend_back(layer):
        deep = layer > 0

        def body(g, carry):
            lanes = pl.ds(pl.multiple_of(g * LANES, LANES), LANES)
            if deep:
                dks[:, lanes] = jnp.zeros((ext, LANES), F32)
                dvs[:, lanes] = jnp.zeros((ext, LANES), F32)
            for b in range(nblk):
                rows_b = slice(b * BLOCK, (b + 1) * BLOCK)
                window = slice(b * BLOCK, b * BLOCK + win)
                value = vs[layer, window, lanes]
                da = dacc[rows_b, lanes]
                pieces = []
                total = gsum[b]
                for i in range(per):
                    h = g * per + i
                    part = pl.ds(pl.multiple_of(h * hdim, hdim), hdim)
                    delta = jnp.sum(
                        dat[part, rows_b] * att[layer, part, rows_b], axis=0, keepdims=True
                    )
                    dp = mm_nt(value, da * masks[i])
                    ds = probs[layer, h, b].astype(F32) * (dp - delta)
                    total = total - gam_ref[layer, h] * ds
                    if deep:
                        dsb = ds.astype(BF16)
                        dqt[part, rows_b] = mm(kt[part, window], dsb)
                        pieces.append(dsb)
                gsum[b] = total
                if deep:
                    query = qs[layer, rows_b, lanes]
                    dks[window, lanes] += mm(
                        jnp.concatenate(pieces, axis=1),
                        jnp.concatenate([query * m for m in masks], axis=0),
                    )
                    dvs[window, lanes] += mm(
                        jnp.concatenate([probs[layer, g * per + i, b] for i in range(per)], axis=1),
                        jnp.concatenate([da * m for m in masks], axis=0),
                    )
            return carry

        lax.fori_loop(0, groups, body, 0)

    for layer in reversed(range(layers)):
        if layer == layers - 1:
            advance()
        grad = slopes(layer, grad)
        advance()
        attend_back(layer)
        if layer:
            def into(part):
                return mm_nt((dks[part, :] * scale).astype(BF16), wk[layer]) + mm_nt(
                    dvs[part, :].astype(BF16), wv[layer]
                )

            gsend[0] = into(slice(0, BLOCK)).astype(BF16)
            gsend[1] = into(slice(BLOCK + atoms, ext)).astype(BF16)
            dq = (jnp.transpose(dqt[...]) * scale).astype(BF16)
            start(swap_g)
            dn = into(own) + mm_nt(dq, wq[layer])
            advance()
            received(swap_g)
            head = [grecv[0].astype(F32)] + [None] * (nblk - 1)
            dn_blocks = []
            for b in range(nblk):
                piece = dn[b * BLOCK : (b + 1) * BLOCK]
                if b == 0:
                    piece = piece + grecv[0].astype(F32)
                if b == nblk - 1:
                    piece = piece + grecv[1].astype(F32)
                dn_blocks.append(piece)
            dn = jnp.concatenate(dn_blocks, axis=0).astype(BF16).astype(F32)
            grad = grad + rms_back(xin[layer], gain_a[layer], dn)

    def rows8(ref):
        return jnp.concatenate(
            [ref[...], jnp.ones((1, BLOCK), F32), jnp.zeros((4, BLOCK), F32)], axis=0
        )

    full = [rows8(ref) for ref in rows]
    parts = [jnp.zeros((8, BLOCK), F32) for _ in rows]
    exact = lax.Precision.HIGHEST
    for b in range(nblk):
        fq = full[b + 1]
        for s in range(3):
            j = b + s
            g = gsum[b, s * BLOCK : (s + 1) * BLOCK, :]
            to_q = jnp.dot(full[j], g, precision=exact, preferred_element_type=F32)
            to_k = lax.dot_general(
                fq, g, (((1,), (1,)), ((), ())), precision=exact, preferred_element_type=F32
            )
            parts[b + 1] = parts[b + 1] + 2.0 * (fq * to_q[3:4, :] - to_q)
            parts[j] = parts[j] + 2.0 * (full[j] * to_k[3:4, :] - to_k)
    fsend[0] = parts[0]
    fsend[1] = parts[nblk + 1]
    for b in range(nblk):
        fown[:, b * BLOCK : (b + 1) * BLOCK] = parts[b + 1]
    start(swap_f)
    while done[0] <= steps:
        advance()
    for s in range(steps):
        ecopies[s].wait_send()
    e_ref[0] = jnp.max(esend[steps])
    sent(swap_sp)
    sent(swap_ps)
    sent(swap_xn)
    sent(swap_g)
    received(swap_f)
    fown[:, 0:BLOCK] += frecv[0]
    fown[:, atoms - BLOCK : atoms] += frecv[1]
    f_ref[...] = -fown[0:3, :]
    sent(swap_f)


def solution(mesh):
    chain = mesh.shape["chain"]

    def local(
        species, positions, block_list, embed_table, w_query, w_key, w_value, w_out, w_up, w_down,
        norm_gains, gammas, out_gain, readout,
    ):
        atoms = species.shape[0]
        nblk = atoms // BLOCK
        width = embed_table.shape[1]
        layers, heads = gammas.shape
        ff = w_up.shape[2]
        ext = atoms + 2 * BLOCK
        win = 3 * BLOCK
        steps = chain.bit_length() - 1
        if layers != 2 or chain != 1 << steps:
            raise ValueError("unsupported sizes")
        vmem = pl.BlockSpec(memory_space=pltpu.VMEM)
        smem = pl.BlockSpec(memory_space=pltpu.SMEM)
        anys = pl.BlockSpec(memory_space=pl.ANY)
        V = pltpu.VMEM
        energy, forces = pl.pallas_call(
            functools.partial(kernel, chain, nblk, layers, heads),
            out_shape=(
                jax.ShapeDtypeStruct((1,), F32),
                jax.ShapeDtypeStruct((3, atoms), F32),
            ),
            in_specs=[vmem, vmem, smem, smem, vmem, vmem, vmem, vmem] + [anys] * 6,
            out_specs=(smem, vmem),
            scratch_shapes=[
                V((layers, width, width), BF16), V((layers, width, width), BF16),
                V((layers, width, width), BF16), V((layers, width, width), BF16),
                V((layers, width, ff), BF16), V((layers, ff, width), BF16),
                V((1, BLOCK), jnp.int32), V((1, BLOCK), jnp.int32),
                V((3, BLOCK), F32), V((3, BLOCK), F32),
                V((layers, ext, width), BF16),
                V((layers, atoms, width), BF16),
                V((layers, ext, width), BF16), V((layers, ext, width), BF16),
                V((width, ext), BF16), V((width, ext), BF16),
                V((layers, heads, nblk, win, BLOCK), BF16),
                V((nblk, win, BLOCK), F32), V((nblk, win, BLOCK), F32),
                V((layers, width, atoms), F32),
                V((layers, atoms, width), F32), V((layers, atoms, width), F32),
                V((layers, atoms, ff), F32),
                V((atoms, width), BF16), V((width, atoms), F32),
                V((width, atoms), F32), V((ext, width), F32), V((ext, width), F32),
                V((2, BLOCK, width), BF16), V((2, BLOCK, width), BF16),
                V((2, 8, BLOCK), F32), V((2, 8, BLOCK), F32), V((8, atoms), F32),
                V((steps + 1, 8, LANES), F32), V((steps + 1, 8, LANES), F32),
                pltpu.SemaphoreType.DMA((layers, 6)),
                pltpu.SemaphoreType.DMA((5, 2)), pltpu.SemaphoreType.DMA((5, 2)),
                pltpu.SemaphoreType.DMA((steps + 1,)), pltpu.SemaphoreType.DMA((steps + 1,)),
            ],
            compiler_params=pltpu.CompilerParams(
                collective_id=0, has_side_effects=True, vmem_limit_bytes=60 * 1024 * 1024
            ),
        )(
            species.reshape(1, atoms), positions, block_list, gammas, norm_gains,
            out_gain.reshape(1, width), readout.reshape(1, width), embed_table,
            w_query, w_key, w_value, w_out, w_up, w_down,
        )
        return energy, forces

    shard = P(("frames", "chain"))
    return jax.shard_map(
        local,
        mesh=mesh,
        in_specs=(shard, P(None, ("frames", "chain")), P(("frames", "chain"), None)) + (P(),) * 11,
        out_specs=(P("frames"), P(None, ("frames", "chain"))),
        check_vma=False,
    )
```

```python
import functools
import math

import jax
import jax.numpy as jnp
from jax import lax
from jax.experimental import pallas as pl
from jax.experimental.pallas import tpu as pltpu
from jax.sharding import PartitionSpec as P

MESH = pl.DeviceIdType.MESH
BLOCK = 128
LANES = 128
FAR = 1e30
EPS = 1e-06
GELU_A = math.sqrt(2.0 / math.pi)
GELU_B = 0.044715
F32 = jnp.float32
BF16 = jnp.bfloat16


def mm(a, b):
    return jnp.dot(a, b, preferred_element_type=F32)


def mm_nt(a, b):
    return lax.dot_general(a, b, (((1,), (1,)), ((), ())), preferred_element_type=F32)


def mm_tn(a, b):
    return lax.dot_general(a, b, (((0,), (0,)), ((), ())), preferred_element_type=F32)


def inv_rms(x):
    return lax.rsqrt(jnp.mean(x * x, axis=-1, keepdims=True) + EPS)


def rms_back(x, gain, dy):
    r = inv_rms(x)
    gy = gain * dy
    return r * gy - x * (r * r * r * jnp.mean(x * gy, axis=-1, keepdims=True))


def gelu_and_slope(x):
    sq = x * x
    h = 0.5 + 0.5 * jnp.tanh(x * (GELU_A + (GELU_A * GELU_B) * sq))
    u = x * h
    return u, h + u * (1.0 - h) * (2.0 * GELU_A + (6.0 * GELU_A * GELU_B) * sq)


def kernel(
    chain, nblk, layers, heads,
    spec_ref, pos_ref, blk_ref, gam_ref, gains_ref, og_ref, ro_ref, table_ref,
    wq_any, wk_any, wv_any, wo_any, wu_any, wd_any,
    e_ref, f_ref,
    wq, wk, wv, wo, wu, wd,
    sp_lo, sp_hi, ps_lo, ps_hi,
    xn, qs, ks, vs, kt, vt, probs, dist, gsum,
    att, xin, xmid, pre, dacc, dat, dqt, dks, dvs,
    gsend, grecv, fsend, frecv, fown, esend, erecv, scores, dsc, invs,
    wsem, ssem, rsem, essem, ersem,
):
    atoms = pos_ref.shape[1]
    width = table_ref.shape[1]
    nspec = table_ref.shape[0]
    hdim = width // heads
    per = LANES // hdim
    groups = width // LANES
    win = 3 * BLOCK
    ext = atoms + 2 * BLOCK
    own = slice(BLOCK, BLOCK + atoms)
    scale = hdim ** -0.5
    qscale = scale * math.log2(math.e)
    me = lax.axis_index("chain")
    has_l = me > 0
    has_r = me < chain - 1
    left = lax.rem(me + chain - 1, chain)
    right = lax.rem(me + 1, chain)
    steps = chain.bit_length() - 1

    loads = {}
    for layer in range(layers):
        for i, (src, dst) in enumerate(
            ((wk_any, wk), (wv_any, wv), (wq_any, wq), (wo_any, wo), (wu_any, wu), (wd_any, wd))
        ):
            copy = pltpu.make_async_copy(src.at[layer], dst.at[layer], wsem.at[layer, i])
            copy.start()
            loads[layer, i] = copy

    barrier = pltpu.get_barrier_semaphore()
    partners = []
    for s in range(steps):
        bit = 1 << s
        partners.append(me + bit - 2 * bit * lax.rem(lax.div(me, bit), 2))

    def greet(to):
        pl.semaphore_signal(barrier, inc=1, device_id={"chain": to}, device_id_type=MESH)

    for partner in partners[1:]:
        greet(partner)

    @pl.when(has_l)
    def _():
        greet(left)

    @pl.when(has_r)
    def _():
        greet(right)

    pl.semaphore_wait(
        barrier, max(0, steps - 1) + has_l.astype(jnp.int32) + has_r.astype(jnp.int32)
    )

    def swap(slot, first, last, high, low):
        to_left = pltpu.make_async_remote_copy(
            src_ref=first, dst_ref=high, send_sem=ssem.at[slot, 0], recv_sem=rsem.at[slot, 0],
            device_id={"chain": left}, device_id_type=MESH,
        )
        to_right = pltpu.make_async_remote_copy(
            src_ref=last, dst_ref=low, send_sem=ssem.at[slot, 1], recv_sem=rsem.at[slot, 1],
            device_id={"chain": right}, device_id_type=MESH,
        )
        return to_left, to_right

    def start(pair):
        pl.when(has_l)(pair[0].start)
        pl.when(has_r)(pair[1].start)

    def received(pair):
        pl.when(has_r)(pair[0].wait_recv)
        pl.when(has_l)(pair[1].wait_recv)

    def sent(pair):
        pl.when(has_l)(pair[0].wait_send)
        pl.when(has_r)(pair[1].wait_send)

    head_first = pl.ds(0, BLOCK)
    head_last = pl.ds(atoms - BLOCK, BLOCK)
    swap_sp = swap(0, spec_ref.at[:, head_first], spec_ref.at[:, head_last], sp_hi, sp_lo)
    swap_ps = swap(1, pos_ref.at[:, head_first], pos_ref.at[:, head_last], ps_hi, ps_lo)
    start(swap_sp)
    start(swap_ps)
    swap_xn = swap(
        2,
        xn.at[1, pl.ds(BLOCK, BLOCK)], xn.at[1, pl.ds(atoms, BLOCK)],
        xn.at[1, pl.ds(BLOCK + atoms, BLOCK)], xn.at[1, pl.ds(0, BLOCK)],
    )
    swap_g = swap(3, gsend.at[0], gsend.at[1], grecv.at[1], grecv.at[0])
    swap_f = swap(4, fsend.at[0], fsend.at[1], frecv.at[1], frecv.at[0])

    @pl.when(me == 0)
    def _():
        sp_lo[...] = jnp.zeros_like(sp_lo)
        ps_lo[...] = jnp.zeros_like(ps_lo)
        xn[1, 0:BLOCK, :] = jnp.zeros((BLOCK, width), BF16)
        grecv[0] = jnp.zeros((BLOCK, width), BF16)
        frecv[0] = jnp.zeros((8, BLOCK), F32)

    @pl.when(me == chain - 1)
    def _():
        sp_hi[...] = jnp.zeros_like(sp_hi)
        ps_hi[...] = jnp.zeros_like(ps_hi)
        xn[1, BLOCK + atoms : ext, :] = jnp.zeros((BLOCK, width), BF16)
        grecv[1] = jnp.zeros((BLOCK, width), BF16)
        frecv[1] = jnp.zeros((8, BLOCK), F32)

    table = table_ref[...]

    def embed(row):
        count = row.shape[1]
        hot = (lax.broadcasted_iota(jnp.int32, (nspec, count), 0) == row).astype(F32).astype(BF16)
        return mm_tn(hot, table)

    def norm(x, gain):
        return (x * inv_rms(x) * gain).astype(BF16)

    gain_a = [gains_ref[layer, 0:1, :] for layer in range(layers)]
    gain_b = [gains_ref[layer, 1:2, :] for layer in range(layers)]

    state = embed(spec_ref[...])
    xn[0, own, :] = norm(state, gain_a[0])
    received(swap_sp)
    xn[0, 0:BLOCK, :] = norm(embed(sp_lo[...]), gain_a[0])
    xn[0, BLOCK + atoms : ext, :] = norm(embed(sp_hi[...]), gain_a[0])
    received(swap_ps)

    rows = [ps_lo] + [pos_ref.at[:, pl.ds(b * BLOCK, BLOCK)] for b in range(nblk)] + [ps_hi]
    columns = [
        [jnp.transpose(jnp.broadcast_to(ref[c : c + 1, :], (BLOCK, BLOCK))) for c in range(3)]
        for ref in rows
    ]
    for b in range(nblk):
        for s in range(3):
            total = None
            for c in range(3):
                diff = columns[b + s][c] - rows[b + 1][c : c + 1, :]
                total = diff * diff if total is None else total + diff * diff
            block = blk_ref[b, s]
            listed = jnp.logical_and(block == me * nblk + (b - 1 + s), block >= 0)
            dist[b, s * BLOCK : (s + 1) * BLOCK, :] = jnp.where(listed, total, FAR)

    lane = lax.broadcasted_iota(jnp.int32, (1, LANES), 1)
    masks = [
        jnp.logical_and(lane >= i * hdim, lane < (i + 1) * hdim).astype(F32).astype(BF16)
        for i in range(per)
    ]
    gsum[...] = jnp.zeros_like(gsum)

    def keys_values(layer, part):
        src = xn[layer, part, :]
        k = mm(src, wk[layer])
        v = mm(src, wv[layer])
        ks[layer, part, :] = k.astype(BF16)
        vs[layer, part, :] = v.astype(BF16)
        vt[:, part] = jnp.transpose(v).astype(BF16)
        if layer:
            kt[:, part] = jnp.transpose(k).astype(BF16)

    units = [(b, i) for b in range(nblk) for i in range(per)]
    ones = jnp.ones((16, win), BF16)

    def attend(layer):
        def body(g, carry):
            lanes = pl.ds(pl.multiple_of(g * LANES, LANES), LANES)
            peaks = []
            for u, (b, i) in enumerate(units):
                key = ks[layer, b * BLOCK : b * BLOCK + win, lanes]
                query = qs[layer, b * BLOCK : (b + 1) * BLOCK, lanes]
                slope = gam_ref[layer, g * per + i] * math.log2(math.e)
                score = mm_nt(key, query * masks[i]) - slope * dist[b]
                scores[u] = score
                peaks.append(jnp.max(score, axis=0, keepdims=True))
            for u, (b, i) in enumerate(units):
                probs[layer, g * per + i, b] = jnp.exp2(scores[u] - peaks[u]).astype(BF16)
            for u, (b, i) in enumerate(units):
                h = g * per + i
                part = pl.ds(pl.multiple_of(h * hdim, hdim), hdim)
                cols = slice(b * BLOCK, (b + 1) * BLOCK)
                value = jnp.concatenate([vt[part, b * BLOCK : b * BLOCK + win], ones], axis=0)
                mixed = mm(value, probs[layer, h, b])
                inv = 1.0 / mixed[hdim : hdim + 1, :]
                invs[layer, h, :, cols] = inv
                att[layer, part, cols] = mixed[0:hdim, :] * inv
            return carry

        lax.fori_loop(0, groups, body, 0)

    for layer in range(layers):
        xin[layer] = state
        if layer == 0:
            loads[layer, 0].wait()
            loads[layer, 1].wait()
            keys_values(layer, slice(0, ext))
            loads[layer, 2].wait()
            qs[layer] = (mm(xn[layer, own, :], wq[layer]) * qscale).astype(BF16)
        else:
            xn[layer, own, :] = norm(state, gain_a[layer])
            loads[layer, 0].wait()
            loads[layer, 1].wait()
            loads[layer, 2].wait()
            start(swap_xn)
            qs[layer] = (mm(xn[layer, own, :], wq[layer]) * qscale).astype(BF16)
            keys_values(layer, own)
            received(swap_xn)
            keys_values(layer, slice(0, BLOCK))
            keys_values(layer, slice(BLOCK + atoms, ext))
        attend(layer)
        loads[layer, 3].wait()
        mid = state + mm(jnp.transpose(att[layer]).astype(BF16), wo[layer])
        xmid[layer] = mid
        loads[layer, 4].wait()
        hidden = mm(norm(mid, gain_b[layer]), wu[layer])
        hidden, pre[layer] = gelu_and_slope(hidden)
        loads[layer, 5].wait()
        state = mid + mm(hidden.astype(BF16), wd[layer])

    r = inv_rms(state)
    gy = og_ref[...] * ro_ref[...]
    energy = jnp.sum(state * r * gy)
    grad = r * gy - state * (r * r * r * jnp.mean(state * gy, axis=-1, keepdims=True))

    ecopies = [
        pltpu.make_async_remote_copy(
            src_ref=esend.at[s], dst_ref=erecv.at[s], send_sem=essem.at[s], recv_sem=ersem.at[s],
            device_id={"chain": partners[s]}, device_id_type=MESH,
        )
        for s in range(steps)
    ]
    esend[0] = jnp.broadcast_to(energy, (8, LANES))
    done = [0]

    def advance(last=False):
        s = done[0]
        if s > 0 and s <= steps:
            ecopies[s - 1].wait_recv()
            esend[s] = esend[s - 1] + erecv[s - 1]
        if s < steps:
            ecopies[s].start()
        done[0] = s + 1

    def slopes(layer, grad):
        du = mm_nt(grad.astype(BF16), wd[layer]).astype(BF16).astype(F32)
        dpre = (du * pre[layer]).astype(BF16)
        dm = mm_nt(dpre, wu[layer]).astype(BF16).astype(F32)
        grad = grad + rms_back(xmid[layer], gain_b[layer], dm)
        da = mm_nt(grad.astype(BF16), wo[layer])
        da = jnp.transpose(da)
        for h in range(heads):
            part = slice(h * hdim, (h + 1) * hdim)
            dat[part, :] = da[part, :] * invs[layer, h]
        dacc[...] = jnp.transpose(dat[...]).astype(BF16)
        return grad

    def attend_back(layer):
        deep = layer > 0

        def body(g, carry):
            lanes = pl.ds(pl.multiple_of(g * LANES, LANES), LANES)
            if deep:
                dks[:, lanes] = jnp.zeros((ext, LANES), F32)
                dvs[:, lanes] = jnp.zeros((ext, LANES), F32)
            for b in range(nblk):
                rows_b = slice(b * BLOCK, (b + 1) * BLOCK)
                window = slice(b * BLOCK, b * BLOCK + win)
                value = vs[layer, window, lanes]
                da = dacc[rows_b, lanes]
                total = gsum[b]
                for i in range(per):
                    h = g * per + i
                    part = pl.ds(pl.multiple_of(h * hdim, hdim), hdim)
                    delta = jnp.sum(
                        dat[part, rows_b] * att[layer, part, rows_b], axis=0, keepdims=True
                    )
                    dp = mm_nt(value, da * masks[i])
                    ds = probs[layer, h, b].astype(F32) * (dp - delta)
                    total = total - gam_ref[layer, h] * ds
                    if deep:
                        dsc[b, :, i * BLOCK : (i + 1) * BLOCK] = ds.astype(BF16)
                gsum[b] = total
            if deep:
                for b in range(nblk):
                    rows_b = slice(b * BLOCK, (b + 1) * BLOCK)
                    window = slice(b * BLOCK, b * BLOCK + win)
                    query = qs[layer, rows_b, lanes]
                    da = dacc[rows_b, lanes]
                    dks[window, lanes] += mm(
                        dsc[b], jnp.concatenate([query * m for m in masks], axis=0)
                    )
                    dvs[window, lanes] += mm(
                        jnp.concatenate([probs[layer, g * per + i, b] for i in range(per)], axis=1),
                        jnp.concatenate([da * m for m in masks], axis=0),
                    )
                    for i in range(per):
                        part = pl.ds(pl.multiple_of((g * per + i) * hdim, hdim), hdim)
                        dqt[part, rows_b] = mm(
                            kt[part, window], dsc[b, :, i * BLOCK : (i + 1) * BLOCK]
                        )
            return carry

        lax.fori_loop(0, groups, body, 0)

    for layer in reversed(range(layers)):
        if layer == layers - 1:
            advance()
        grad = slopes(layer, grad)
        advance()
        attend_back(layer)
        if layer:
            def into(part):
                return mm_nt((dks[part, :] * math.log(2.0)).astype(BF16), wk[layer]) + mm_nt(
                    dvs[part, :].astype(BF16), wv[layer]
                )

            gsend[0] = into(slice(0, BLOCK)).astype(BF16)
            gsend[1] = into(slice(BLOCK + atoms, ext)).astype(BF16)
            dq = (jnp.transpose(dqt[...]) * scale).astype(BF16)
            start(swap_g)
            dn = into(own) + mm_nt(dq, wq[layer])
            advance()
            received(swap_g)
            dn_blocks = []
            for b in range(nblk):
                piece = dn[b * BLOCK : (b + 1) * BLOCK]
                if b == 0:
                    piece = piece + grecv[0].astype(F32)
                if b == nblk - 1:
                    piece = piece + grecv[1].astype(F32)
                dn_blocks.append(piece)
            dn = jnp.concatenate(dn_blocks, axis=0).astype(BF16).astype(F32)
            grad = grad + rms_back(xin[layer], gain_a[layer], dn)

    def rows8(ref):
        return jnp.concatenate(
            [ref[...], jnp.ones((1, BLOCK), F32), jnp.zeros((4, BLOCK), F32)], axis=0
        )

    full = [rows8(ref) for ref in rows]
    parts = [jnp.zeros((8, BLOCK), F32) for _ in rows]
    exact = lax.Precision.HIGHEST
    for b in range(nblk):
        fq = full[b + 1]
        for s in range(3):
            j = b + s
            g = gsum[b, s * BLOCK : (s + 1) * BLOCK, :]
            to_q = jnp.dot(full[j], g, precision=exact, preferred_element_type=F32)
            to_k = lax.dot_general(
                fq, g, (((1,), (1,)), ((), ())), precision=exact, preferred_element_type=F32
            )
            parts[b + 1] = parts[b + 1] + 2.0 * (fq * to_q[3:4, :] - to_q)
            parts[j] = parts[j] + 2.0 * (full[j] * to_k[3:4, :] - to_k)
    fsend[0] = parts[0]
    fsend[1] = parts[nblk + 1]
    for b in range(nblk):
        fown[:, b * BLOCK : (b + 1) * BLOCK] = parts[b + 1]
    start(swap_f)
    while done[0] <= steps:
        advance()
    for s in range(steps):
        ecopies[s].wait_send()
    e_ref[0] = jnp.max(esend[steps])
    sent(swap_sp)
    sent(swap_ps)
    sent(swap_xn)
    sent(swap_g)
    received(swap_f)
    fown[:, 0:BLOCK] += frecv[0]
    fown[:, atoms - BLOCK : atoms] += frecv[1]
    f_ref[...] = -fown[0:3, :]
    sent(swap_f)


def solution(mesh):
    chain = mesh.shape["chain"]

    def local(
        species, positions, block_list, embed_table, w_query, w_key, w_value, w_out, w_up, w_down,
        norm_gains, gammas, out_gain, readout,
    ):
        atoms = species.shape[0]
        nblk = atoms // BLOCK
        width = embed_table.shape[1]
        layers, heads = gammas.shape
        ff = w_up.shape[2]
        ext = atoms + 2 * BLOCK
        win = 3 * BLOCK
        steps = chain.bit_length() - 1
        if layers != 2 or chain != 1 << steps:
            raise ValueError("unsupported sizes")
        vmem = pl.BlockSpec(memory_space=pltpu.VMEM)
        smem = pl.BlockSpec(memory_space=pltpu.SMEM)
        anys = pl.BlockSpec(memory_space=pl.ANY)
        V = pltpu.VMEM
        energy, forces = pl.pallas_call(
            functools.partial(kernel, chain, nblk, layers, heads),
            out_shape=(
                jax.ShapeDtypeStruct((1,), F32),
                jax.ShapeDtypeStruct((3, atoms), F32),
            ),
            in_specs=[vmem, vmem, smem, smem, vmem, vmem, vmem, vmem] + [anys] * 6,
            out_specs=(smem, vmem),
            scratch_shapes=[
                V((layers, width, width), BF16), V((layers, width, width), BF16),
                V((layers, width, width), BF16), V((layers, width, width), BF16),
                V((layers, width, ff), BF16), V((layers, ff, width), BF16),
                V((1, BLOCK), jnp.int32), V((1, BLOCK), jnp.int32),
                V((3, BLOCK), F32), V((3, BLOCK), F32),
                V((layers, ext, width), BF16),
                V((layers, atoms, width), BF16),
                V((layers, ext, width), BF16), V((layers, ext, width), BF16),
                V((width, ext), BF16), V((width, ext), BF16),
                V((layers, heads, nblk, win, BLOCK), BF16),
                V((nblk, win, BLOCK), F32), V((nblk, win, BLOCK), F32),
                V((layers, width, atoms), F32),
                V((layers, atoms, width), F32), V((layers, atoms, width), F32),
                V((layers, atoms, ff), F32),
                V((atoms, width), BF16), V((width, atoms), F32),
                V((width, atoms), F32), V((ext, width), F32), V((ext, width), F32),
                V((2, BLOCK, width), BF16), V((2, BLOCK, width), BF16),
                V((2, 8, BLOCK), F32), V((2, 8, BLOCK), F32), V((8, atoms), F32),
                V((steps + 1, 8, LANES), F32), V((steps + 1, 8, LANES), F32),
                V((nblk * (LANES * heads // width), win, BLOCK), F32),
                V((nblk, win, LANES * heads // width * BLOCK), BF16),
                V((layers, heads, 1, atoms), F32),
                pltpu.SemaphoreType.DMA((layers, 6)),
                pltpu.SemaphoreType.DMA((5, 2)), pltpu.SemaphoreType.DMA((5, 2)),
                pltpu.SemaphoreType.DMA((steps + 1,)), pltpu.SemaphoreType.DMA((steps + 1,)),
            ],
            compiler_params=pltpu.CompilerParams(
                collective_id=0, has_side_effects=True, vmem_limit_bytes=60 * 1024 * 1024
            ),
        )(
            species.reshape(1, atoms), positions, block_list, gammas, norm_gains,
            out_gain.reshape(1, width), readout.reshape(1, width), embed_table,
            w_query, w_key, w_value, w_out, w_up, w_down,
        )
        return energy, forces

    shard = P(("frames", "chain"))
    return jax.shard_map(
        local,
        mesh=mesh,
        in_specs=(shard, P(None, ("frames", "chain")), P(("frames", "chain"), None)) + (P(),) * 11,
        out_specs=(P("frames"), P(None, ("frames", "chain"))),
        check_vma=False,
    )
```

```python
import functools
import math

import jax
import jax.numpy as jnp
from jax import lax
from jax.experimental import pallas as pl
from jax.experimental.pallas import tpu as pltpu
from jax.sharding import PartitionSpec as P

MESH = pl.DeviceIdType.MESH
BLOCK = 128
LANES = 128
FAR = 1e30
EPS = 1e-06
GELU_A = math.sqrt(2.0 / math.pi)
GELU_B = 0.044715
F32 = jnp.float32
BF16 = jnp.bfloat16


def mm(a, b):
    return jnp.dot(a, b, preferred_element_type=F32)


def mm_nt(a, b):
    return lax.dot_general(a, b, (((1,), (1,)), ((), ())), preferred_element_type=F32)


def mm_tn(a, b):
    return lax.dot_general(a, b, (((0,), (0,)), ((), ())), preferred_element_type=F32)


def inv_rms(x):
    return lax.rsqrt(jnp.mean(x * x, axis=-1, keepdims=True) + EPS)


def rms_back(x, gain, dy):
    r = inv_rms(x)
    gy = gain * dy
    return r * gy - x * (r * r * r * jnp.mean(x * gy, axis=-1, keepdims=True))


def gelu_and_slope(x):
    sq = x * x
    h = 0.5 + 0.5 * jnp.tanh(x * (GELU_A + (GELU_A * GELU_B) * sq))
    u = x * h
    return u, h + u * (1.0 - h) * (2.0 * GELU_A + (6.0 * GELU_A * GELU_B) * sq)


def kernel(
    chain, nblk, layers, heads,
    spec_ref, pos_ref, blk_ref, gam_ref, gains_ref, og_ref, ro_ref, table_ref,
    wq_any, wk_any, wv_any, wo_any, wu_any, wd_any,
    e_ref, f_ref,
    wq, wk, wv, wo, wu, wd,
    sp_lo, sp_hi, ps_lo, ps_hi,
    xn, qs, ks, vs, kt, vt, probs, dist, gsum,
    att, xin, xmid, pre, dacc, dat, dqt, dks, dvs,
    gsend, grecv, fsend, frecv, fown, esend, erecv, scores, dsc, invs,
    wsem, ssem, rsem, essem, ersem,
):
    atoms = pos_ref.shape[1]
    width = table_ref.shape[1]
    nspec = table_ref.shape[0]
    hdim = width // heads
    per = LANES // hdim
    groups = width // LANES
    win = 3 * BLOCK
    ext = atoms + 2 * BLOCK
    own = slice(BLOCK, BLOCK + atoms)
    scale = hdim ** -0.5
    qscale = scale * math.log2(math.e)
    me = lax.axis_index("chain")
    has_l = me > 0
    has_r = me < chain - 1
    left = lax.rem(me + chain - 1, chain)
    right = lax.rem(me + 1, chain)
    steps = chain.bit_length() - 1

    loads = {}
    for layer in range(layers):
        for i, (src, dst) in enumerate(
            ((wk_any, wk), (wv_any, wv), (wq_any, wq), (wo_any, wo), (wu_any, wu), (wd_any, wd))
        ):
            copy = pltpu.make_async_copy(src.at[layer], dst.at[layer], wsem.at[layer, i])
            copy.start()
            loads[layer, i] = copy

    barrier = pltpu.get_barrier_semaphore()
    partners = []
    for s in range(steps):
        bit = 1 << s
        partners.append(me + bit - 2 * bit * lax.rem(lax.div(me, bit), 2))

    def greet(to):
        pl.semaphore_signal(barrier, inc=1, device_id={"chain": to}, device_id_type=MESH)

    for partner in partners[1:]:
        greet(partner)

    @pl.when(has_l)
    def _():
        greet(left)

    @pl.when(has_r)
    def _():
        greet(right)

    pl.semaphore_wait(
        barrier, max(0, steps - 1) + has_l.astype(jnp.int32) + has_r.astype(jnp.int32)
    )

    def swap(slot, first, last, high, low):
        to_left = pltpu.make_async_remote_copy(
            src_ref=first, dst_ref=high, send_sem=ssem.at[slot, 0], recv_sem=rsem.at[slot, 0],
            device_id={"chain": left}, device_id_type=MESH,
        )
        to_right = pltpu.make_async_remote_copy(
            src_ref=last, dst_ref=low, send_sem=ssem.at[slot, 1], recv_sem=rsem.at[slot, 1],
            device_id={"chain": right}, device_id_type=MESH,
        )
        return to_left, to_right

    def start(pair):
        pl.when(has_l)(pair[0].start)
        pl.when(has_r)(pair[1].start)

    def received(pair):
        pl.when(has_r)(pair[0].wait_recv)
        pl.when(has_l)(pair[1].wait_recv)

    def sent(pair):
        pl.when(has_l)(pair[0].wait_send)
        pl.when(has_r)(pair[1].wait_send)

    head_first = pl.ds(0, BLOCK)
    head_last = pl.ds(atoms - BLOCK, BLOCK)
    swap_sp = swap(0, spec_ref.at[:, head_first], spec_ref.at[:, head_last], sp_hi, sp_lo)
    swap_ps = swap(1, pos_ref.at[:, head_first], pos_ref.at[:, head_last], ps_hi, ps_lo)
    start(swap_sp)
    start(swap_ps)
    swap_xn = swap(
        2,
        xn.at[1, pl.ds(BLOCK, BLOCK)], xn.at[1, pl.ds(atoms, BLOCK)],
        xn.at[1, pl.ds(BLOCK + atoms, BLOCK)], xn.at[1, pl.ds(0, BLOCK)],
    )
    swap_g = swap(3, gsend.at[0], gsend.at[1], grecv.at[1], grecv.at[0])
    swap_f = swap(4, fsend.at[0], fsend.at[1], frecv.at[1], frecv.at[0])

    @pl.when(me == 0)
    def _():
        sp_lo[...] = jnp.zeros_like(sp_lo)
        ps_lo[...] = jnp.zeros_like(ps_lo)
        xn[1, 0:BLOCK, :] = jnp.zeros((BLOCK, width), BF16)
        grecv[0] = jnp.zeros((BLOCK, width), BF16)
        frecv[0] = jnp.zeros((8, BLOCK), F32)

    @pl.when(me == chain - 1)
    def _():
        sp_hi[...] = jnp.zeros_like(sp_hi)
        ps_hi[...] = jnp.zeros_like(ps_hi)
        xn[1, BLOCK + atoms : ext, :] = jnp.zeros((BLOCK, width), BF16)
        grecv[1] = jnp.zeros((BLOCK, width), BF16)
        frecv[1] = jnp.zeros((8, BLOCK), F32)

    table = table_ref[...]

    def embed(row):
        count = row.shape[1]
        hot = (lax.broadcasted_iota(jnp.int32, (nspec, count), 0) == row).astype(F32).astype(BF16)
        return mm_tn(hot, table)

    def norm(x, gain):
        return (x * inv_rms(x) * gain).astype(BF16)

    gain_a = [gains_ref[layer, 0:1, :] for layer in range(layers)]
    gain_b = [gains_ref[layer, 1:2, :] for layer in range(layers)]

    state = embed(spec_ref[...])
    xn[0, own, :] = norm(state, gain_a[0])
    received(swap_sp)
    xn[0, 0:BLOCK, :] = norm(embed(sp_lo[...]), gain_a[0])
    xn[0, BLOCK + atoms : ext, :] = norm(embed(sp_hi[...]), gain_a[0])
    received(swap_ps)

    rows = [ps_lo] + [pos_ref.at[:, pl.ds(b * BLOCK, BLOCK)] for b in range(nblk)] + [ps_hi]
    columns = [
        [jnp.transpose(jnp.broadcast_to(ref[c : c + 1, :], (BLOCK, BLOCK))) for c in range(3)]
        for ref in rows
    ]
    for b in range(nblk):
        for s in range(3):
            total = None
            for c in range(3):
                diff = columns[b + s][c] - rows[b + 1][c : c + 1, :]
                total = diff * diff if total is None else total + diff * diff
            block = blk_ref[b, s]
            listed = jnp.logical_and(block == me * nblk + (b - 1 + s), block >= 0)
            dist[b, s * BLOCK : (s + 1) * BLOCK, :] = jnp.where(listed, total, FAR)

    lane = lax.broadcasted_iota(jnp.int32, (1, LANES), 1)
    masks = [
        jnp.logical_and(lane >= i * hdim, lane < (i + 1) * hdim).astype(F32).astype(BF16)
        for i in range(per)
    ]
    gsum[...] = jnp.zeros_like(gsum)

    def keys_values(layer, part):
        src = xn[layer, part, :]
        k = mm(src, wk[layer])
        v = mm(src, wv[layer])
        ks[layer, part, :] = k.astype(BF16)
        vs[layer, part, :] = v.astype(BF16)
        vt[:, part] = jnp.transpose(v).astype(BF16)
        if layer:
            kt[:, part] = jnp.transpose(k).astype(BF16)

    units = [(b, i) for b in range(nblk) for i in range(per)]
    ones = jnp.ones((16, win), BF16)

    def attend(layer):
        def body(g, carry):
            lanes = pl.ds(pl.multiple_of(g * LANES, LANES), LANES)
            peaks = []
            for u, (b, i) in enumerate(units):
                key = ks[layer, b * BLOCK : b * BLOCK + win, lanes]
                query = qs[layer, b * BLOCK : (b + 1) * BLOCK, lanes]
                slope = gam_ref[layer, g * per + i] * math.log2(math.e)
                score = mm_nt(key, query * masks[i]) * qscale - slope * dist[b]
                scores[u] = score
                peaks.append(jnp.max(score, axis=0, keepdims=True))
            for u, (b, i) in enumerate(units):
                probs[layer, g * per + i, b] = jnp.exp2(scores[u] - peaks[u]).astype(BF16)
            for u, (b, i) in enumerate(units):
                h = g * per + i
                part = pl.ds(pl.multiple_of(h * hdim, hdim), hdim)
                cols = slice(b * BLOCK, (b + 1) * BLOCK)
                value = jnp.concatenate([vt[part, b * BLOCK : b * BLOCK + win], ones], axis=0)
                mixed = mm(value, probs[layer, h, b])
                inv = 1.0 / mixed[hdim : hdim + 1, :]
                invs[layer, h, :, cols] = inv
                att[layer, part, cols] = mixed[0:hdim, :] * inv
            return carry

        lax.fori_loop(0, groups, body, 0)

    for layer in range(layers):
        xin[layer] = state
        if layer == 0:
            loads[layer, 0].wait()
            loads[layer, 1].wait()
            keys_values(layer, slice(0, ext))
            loads[layer, 2].wait()
            qs[layer] = mm(xn[layer, own, :], wq[layer]).astype(BF16)
        else:
            xn[layer, own, :] = norm(state, gain_a[layer])
            loads[layer, 0].wait()
            loads[layer, 1].wait()
            loads[layer, 2].wait()
            start(swap_xn)
            qs[layer] = mm(xn[layer, own, :], wq[layer]).astype(BF16)
            keys_values(layer, own)
            received(swap_xn)
            keys_values(layer, slice(0, BLOCK))
            keys_values(layer, slice(BLOCK + atoms, ext))
        attend(layer)
        loads[layer, 3].wait()
        mid = state + mm(jnp.transpose(att[layer]).astype(BF16), wo[layer])
        xmid[layer] = mid
        loads[layer, 4].wait()
        hidden = mm(norm(mid, gain_b[layer]), wu[layer])
        hidden, pre[layer] = gelu_and_slope(hidden)
        loads[layer, 5].wait()
        state = mid + mm(hidden.astype(BF16), wd[layer])

    r = inv_rms(state)
    gy = og_ref[...] * ro_ref[...]
    energy = jnp.sum(state * r * gy)
    grad = r * gy - state * (r * r * r * jnp.mean(state * gy, axis=-1, keepdims=True))

    ecopies = [
        pltpu.make_async_remote_copy(
            src_ref=esend.at[s], dst_ref=erecv.at[s], send_sem=essem.at[s], recv_sem=ersem.at[s],
            device_id={"chain": partners[s]}, device_id_type=MESH,
        )
        for s in range(steps)
    ]
    esend[0] = jnp.broadcast_to(energy, (8, LANES))
    done = [0]

    def advance(last=False):
        s = done[0]
        if s > 0 and s <= steps:
            ecopies[s - 1].wait_recv()
            esend[s] = esend[s - 1] + erecv[s - 1]
        if s < steps:
            ecopies[s].start()
        done[0] = s + 1

    def slopes(layer, grad):
        du = mm_nt(grad.astype(BF16), wd[layer]).astype(BF16).astype(F32)
        dpre = (du * pre[layer]).astype(BF16)
        dm = mm_nt(dpre, wu[layer]).astype(BF16).astype(F32)
        grad = grad + rms_back(xmid[layer], gain_b[layer], dm)
        da = mm_nt(grad.astype(BF16), wo[layer])
        da = jnp.transpose(da)
        for h in range(heads):
            part = slice(h * hdim, (h + 1) * hdim)
            dat[part, :] = da[part, :] * invs[layer, h]
        dacc[...] = jnp.transpose(dat[...]).astype(BF16)
        return grad

    def attend_back(layer):
        deep = layer > 0

        def body(g, carry):
            lanes = pl.ds(pl.multiple_of(g * LANES, LANES), LANES)
            if deep:
                dks[:, lanes] = jnp.zeros((ext, LANES), F32)
                dvs[:, lanes] = jnp.zeros((ext, LANES), F32)
            for b in range(nblk):
                rows_b = slice(b * BLOCK, (b + 1) * BLOCK)
                window = slice(b * BLOCK, b * BLOCK + win)
                value = vs[layer, window, lanes]
                da = dacc[rows_b, lanes]
                total = gsum[b]
                for i in range(per):
                    h = g * per + i
                    part = pl.ds(pl.multiple_of(h * hdim, hdim), hdim)
                    delta = jnp.sum(
                        dat[part, rows_b] * att[layer, part, rows_b], axis=0, keepdims=True
                    )
                    dp = mm_nt(value, da * masks[i])
                    ds = probs[layer, h, b].astype(F32) * (dp - delta)
                    total = total - gam_ref[layer, h] * ds
                    if deep:
                        dsc[b, :, i * BLOCK : (i + 1) * BLOCK] = ds.astype(BF16)
                gsum[b] = total
            if deep:
                for b in range(nblk):
                    rows_b = slice(b * BLOCK, (b + 1) * BLOCK)
                    window = slice(b * BLOCK, b * BLOCK + win)
                    query = qs[layer, rows_b, lanes]
                    da = dacc[rows_b, lanes]
                    dks[window, lanes] += mm(
                        dsc[b], jnp.concatenate([query * m for m in masks], axis=0)
                    )
                    dvs[window, lanes] += mm(
                        jnp.concatenate([probs[layer, g * per + i, b] for i in range(per)], axis=1),
                        jnp.concatenate([da * m for m in masks], axis=0),
                    )
                    for i in range(per):
                        part = pl.ds(pl.multiple_of((g * per + i) * hdim, hdim), hdim)
                        dqt[part, rows_b] = mm(
                            kt[part, window], dsc[b, :, i * BLOCK : (i + 1) * BLOCK]
                        )
            return carry

        lax.fori_loop(0, groups, body, 0)

    for layer in reversed(range(layers)):
        if layer == layers - 1:
            advance()
        grad = slopes(layer, grad)
        advance()
        attend_back(layer)
        if layer:
            def into(part):
                return mm_nt((dks[part, :] * scale).astype(BF16), wk[layer]) + mm_nt(
                    dvs[part, :].astype(BF16), wv[layer]
                )

            gsend[0] = into(slice(0, BLOCK)).astype(BF16)
            gsend[1] = into(slice(BLOCK + atoms, ext)).astype(BF16)
            dq = (jnp.transpose(dqt[...]) * scale).astype(BF16)
            start(swap_g)
            dn = into(own) + mm_nt(dq, wq[layer])
            advance()
            received(swap_g)
            dn_blocks = []
            for b in range(nblk):
                piece = dn[b * BLOCK : (b + 1) * BLOCK]
                if b == 0:
                    piece = piece + grecv[0].astype(F32)
                if b == nblk - 1:
                    piece = piece + grecv[1].astype(F32)
                dn_blocks.append(piece)
            dn = jnp.concatenate(dn_blocks, axis=0).astype(BF16).astype(F32)
            grad = grad + rms_back(xin[layer], gain_a[layer], dn)

    def rows8(ref):
        return jnp.concatenate(
            [ref[...], jnp.ones((1, BLOCK), F32), jnp.zeros((4, BLOCK), F32)], axis=0
        )

    full = [rows8(ref) for ref in rows]
    parts = [jnp.zeros((8, BLOCK), F32) for _ in rows]
    exact = lax.Precision.HIGHEST
    for b in range(nblk):
        fq = full[b + 1]
        for s in range(3):
            j = b + s
            g = gsum[b, s * BLOCK : (s + 1) * BLOCK, :]
            to_q = jnp.dot(full[j], g, precision=exact, preferred_element_type=F32)
            to_k = lax.dot_general(
                fq, g, (((1,), (1,)), ((), ())), precision=exact, preferred_element_type=F32
            )
            parts[b + 1] = parts[b + 1] + 2.0 * (fq * to_q[3:4, :] - to_q)
            parts[j] = parts[j] + 2.0 * (full[j] * to_k[3:4, :] - to_k)
    fsend[0] = parts[0]
    fsend[1] = parts[nblk + 1]
    for b in range(nblk):
        fown[:, b * BLOCK : (b + 1) * BLOCK] = parts[b + 1]
    start(swap_f)
    while done[0] <= steps:
        advance()
    for s in range(steps):
        ecopies[s].wait_send()
    e_ref[0] = jnp.max(esend[steps])
    sent(swap_sp)
    sent(swap_ps)
    sent(swap_xn)
    sent(swap_g)
    received(swap_f)
    fown[:, 0:BLOCK] += frecv[0]
    fown[:, atoms - BLOCK : atoms] += frecv[1]
    f_ref[...] = -fown[0:3, :]
    sent(swap_f)


def solution(mesh):
    chain = mesh.shape["chain"]

    def local(
        species, positions, block_list, embed_table, w_query, w_key, w_value, w_out, w_up, w_down,
        norm_gains, gammas, out_gain, readout,
    ):
        atoms = species.shape[0]
        nblk = atoms // BLOCK
        width = embed_table.shape[1]
        layers, heads = gammas.shape
        ff = w_up.shape[2]
        ext = atoms + 2 * BLOCK
        win = 3 * BLOCK
        steps = chain.bit_length() - 1
        if layers != 2 or chain != 1 << steps:
            raise ValueError("unsupported sizes")
        vmem = pl.BlockSpec(memory_space=pltpu.VMEM)
        smem = pl.BlockSpec(memory_space=pltpu.SMEM)
        anys = pl.BlockSpec(memory_space=pl.ANY)
        V = pltpu.VMEM
        energy, forces = pl.pallas_call(
            functools.partial(kernel, chain, nblk, layers, heads),
            out_shape=(
                jax.ShapeDtypeStruct((1,), F32),
                jax.ShapeDtypeStruct((3, atoms), F32),
            ),
            in_specs=[vmem, vmem, smem, smem, vmem, vmem, vmem, vmem] + [anys] * 6,
            out_specs=(smem, vmem),
            scratch_shapes=[
                V((layers, width, width), BF16), V((layers, width, width), BF16),
                V((layers, width, width), BF16), V((layers, width, width), BF16),
                V((layers, width, ff), BF16), V((layers, ff, width), BF16),
                V((1, BLOCK), jnp.int32), V((1, BLOCK), jnp.int32),
                V((3, BLOCK), F32), V((3, BLOCK), F32),
                V((layers, ext, width), BF16),
                V((layers, atoms, width), BF16),
                V((layers, ext, width), BF16), V((layers, ext, width), BF16),
                V((width, ext), BF16), V((width, ext), BF16),
                V((layers, heads, nblk, win, BLOCK), BF16),
                V((nblk, win, BLOCK), F32), V((nblk, win, BLOCK), F32),
                V((layers, width, atoms), F32),
                V((layers, atoms, width), F32), V((layers, atoms, width), F32),
                V((layers, atoms, ff), F32),
                V((atoms, width), BF16), V((width, atoms), F32),
                V((width, atoms), F32), V((ext, width), F32), V((ext, width), F32),
                V((2, BLOCK, width), BF16), V((2, BLOCK, width), BF16),
                V((2, 8, BLOCK), F32), V((2, 8, BLOCK), F32), V((8, atoms), F32),
                V((steps + 1, 8, LANES), F32), V((steps + 1, 8, LANES), F32),
                V((nblk * (LANES * heads // width), win, BLOCK), F32),
                V((nblk, win, LANES * heads // width * BLOCK), BF16),
                V((layers, heads, 1, atoms), F32),
                pltpu.SemaphoreType.DMA((layers, 6)),
                pltpu.SemaphoreType.DMA((5, 2)), pltpu.SemaphoreType.DMA((5, 2)),
                pltpu.SemaphoreType.DMA((steps + 1,)), pltpu.SemaphoreType.DMA((steps + 1,)),
            ],
            compiler_params=pltpu.CompilerParams(
                collective_id=0, has_side_effects=True, vmem_limit_bytes=60 * 1024 * 1024
            ),
        )(
            species.reshape(1, atoms), positions, block_list, gammas, norm_gains,
            out_gain.reshape(1, width), readout.reshape(1, width), embed_table,
            w_query, w_key, w_value, w_out, w_up, w_down,
        )
        return energy, forces

    shard = P(("frames", "chain"))
    return jax.shard_map(
        local,
        mesh=mesh,
        in_specs=(shard, P(None, ("frames", "chain")), P(("frames", "chain"), None)) + (P(),) * 11,
        out_specs=(P("frames"), P(None, ("frames", "chain"))),
        check_vma=False,
    )
```
